768 devices in a mesh: ctx: 96 (over z, y), fsdp: 8 (over x, core).
Axes of the slice: x: 4, y: 8, z: 12, core: 2. Of those that a mesh axis runs over, the one named last changes fastest.
Arguments:
- values: bfloat16 [8, 12288, 4096], P('fsdp', 'ctx'), may hold values from -6 to 6
- cotangent: bfloat16 [8, 12288, 4096], P('fsdp', 'ctx'), may hold values from -6 to 6
- seg_ids: int32 [8, 12288], P('fsdp', 'ctx'), may hold values from 0 to 3, never falling along the last dimension, each value on 1 to 6144 neighbouring positions
- filters: bfloat16 [256, 128], P('fsdp'), may hold values from -0.5 to 0.5
- skip_gain: bfloat16 [4096], P('fsdp'), may hold values from -4 to 4
Outputs:
- mixed: bfloat16 [8, 12288, 4096], P('fsdp', 'ctx')
- grad_values: bfloat16 [8, 12288, 4096], P('fsdp', 'ctx')
- grad_filters: float32 [256, 128], P('fsdp')
- grad_skip: float32 [4096], P('fsdp')
The draws below stay inside these ranges and needn't reach their ends.
Inputs may be any that keep to these rules, and one draw needn't show every extreme that they name: `seg_ids`: along each stream document numbers start at 0 and never fall; each document covers 1 to 6144 positions, and one covers exactly that many.
All inputs are finite; a program needn't handle non-finite values.
Results may differ from the reference program's by a relative error of at most 0.001.
Values may be sent and summed in bfloat16 or wider, within the bound.
A program may use at most 64 MiB of HBM per device.

```python
import math
import jax
import jax.numpy as jnp
import numpy as np
from jax import lax

CH = 4096
GSIZE = 16
TAPS = 128
TOK_DEV = 128
GROUPS = 256
STREAMS = 8
SEQ = 12288


def with_spikes(result, own_key, source, target, parts, factor):
    def block_of(dim):
        return (jnp.arange(result.shape[dim]) // (result.shape[dim] // parts)).reshape((-1,) + (1,) * (result.ndim - 1 - dim))

    near = jax.random.permutation(own_key, parts)[block_of(target)]
    far = (block_of(target) + parts // 2) % parts
    return jnp.where((block_of(source) == near) | (block_of(source) == far), factor * result, result)


def steps_of(own_key, dims, pieces, least, top_value):
    def one(position, blocks):
        heights = jax.random.uniform(jax.random.fold_in(jax.random.fold_in(own_key, 6), position), (blocks,), jnp.float32, least / len(pieces), top_value / len(pieces))
        return jnp.repeat(jnp.exp(heights), dims[position] // blocks).reshape((-1,) + (1,) * (len(dims) - position - 1))

    factor_of = one(*pieces[0])
    for cut in pieces[1:]:
        factor_of = factor_of * one(*cut)
    return factor_of


def split_up(amount, total, bound, slope):
    portions = [(1 << 20) // math.isqrt(rank ** slope) + 1 for rank in range(2, amount + 1)]
    surplus, given = total - bound - (amount - 1), [1] * (amount - 1)
    while surplus > 0:
        free = [i for i in range(amount - 1) if given[i] < bound]
        whole, budget = sum([portions[i] for i in free]), surplus
        for i in free:
            extra = min(bound - given[i], max(1, budget * portions[i] // whole), surplus)
            given[i] = given[i] + extra
            surplus = surplus - extra
    return np.array([bound] + given)


def uneven(rng, number_of, total, bound, slope):
    if number_of == 2:
        one = jax.random.randint(rng, (), max(1, total - bound), min(bound, total - 1) + 1)
        return jnp.stack([one, total - one])
    lengths = jnp.asarray(split_up(number_of, total, bound, slope), jnp.int32)
    pairs = (number_of - 1) // 2
    giver, receiver = lengths[1:1 + 2 * pairs:2], lengths[2:2 + 2 * pairs:2]
    slack = jnp.minimum(giver - 1, bound - receiver)
    passed = jax.random.randint(jax.random.fold_in(rng, 1), (pairs,), 0, 1 << 20) % (slack + 1)
    lengths = lengths.at[1:1 + 2 * pairs:2].set(giver - passed).at[2:2 + 2 * pairs:2].set(receiver + passed)
    return lengths[jax.random.permutation(jax.random.fold_in(rng, 2), number_of)]


def scatter_about(rng, shape, deviation, bound, shards=(), kind=jnp.bfloat16):
    array = jax.random.normal(rng, shape, jnp.float32) * deviation
    if len(shards) > 0:
        array = steps_of(rng, shape, shards, -0.22, 0.18) * array
    return jnp.clip(array, min=-bound, max=bound).astype(kind)


def gaussian_with(stream_key, extent, scale, bound, pieces, heavy, kind=jnp.bfloat16):
    entries = scale * jax.random.normal(stream_key, extent, jnp.float32)
    if pieces:
        entries = entries * steps_of(stream_key, extent, pieces, -0.22, 0.18)
    return jnp.clip(with_spikes(entries, jax.random.fold_in(stream_key, 3), *heavy), -bound, bound).astype(kind)


def setup_inputs(seed: int = 0) -> dict:
    arg_keys = jax.random.split(jax.random.key(seed), 6)
    values = scatter_about(arg_keys[0], (STREAMS, SEQ, CH), 1.0, 6.0, ((0, 8), (1, 96)))
    cotangent = gaussian_with(arg_keys[1], (STREAMS, SEQ, CH), 1.0, 6.0, ((0, 8), (1, 96)), (0, 2, 8, 2.0))
    seg_ids = jax.vmap(lambda own: jnp.searchsorted(jnp.cumsum(uneven(own, 4, SEQ, SEQ // 2, 2)), jnp.arange(SEQ), side="right"))(jax.random.split(arg_keys[2], STREAMS)).reshape((STREAMS, SEQ)).astype(jnp.int32)
    filters = scatter_about(arg_keys[3], (GROUPS, TAPS), TAPS ** -0.5, 0.5, ((0, 8),))
    skip_gain = scatter_about(arg_keys[4], (CH,), 0.7, 4.0, ((0, 8),))
    return {"values": values, "cotangent": cotangent, "seg_ids": seg_ids, "filters": filters, "skip_gain": skip_gain}


def toeplitz(pattern, rows, width):
    count = pattern.shape[0]
    tiled = jnp.broadcast_to(pattern[:, None, :], (count, rows, width + 1)).reshape(count, rows * (width + 1))
    return tiled[:, :rows * width].reshape(count, rows, width)

def diagonals(matrix, taps):
    count, rows, width = matrix.shape
    flat = jnp.concatenate([matrix.reshape(count, rows * width), jnp.zeros((count, rows), matrix.dtype)], axis=1)
    bands = flat.reshape(count, rows, width + 1)[:, :, 1:taps + 1]
    return lax.optimization_barrier(jnp.sum(bands, axis=1))[:, ::-1]

def reference(values, cotangent, seg_ids, filters, skip_gain):
    width = TAPS + TOK_DEV
    filt = filters.astype(jnp.float32)
    skip = skip_gain.astype(jnp.float32)
    lead = jnp.concatenate([jnp.zeros((GROUPS, 1), jnp.float32), filt[:, ::-1], jnp.zeros((GROUPS, width - TAPS), jnp.float32)], axis=1)
    trail = jnp.concatenate([filt, jnp.zeros((GROUPS, width + 1 - TAPS), jnp.float32)], axis=1)
    forward = toeplitz(lead, TOK_DEV, width)
    backward = toeplitz(trail, TOK_DEV, width)
    zero_rows = jnp.zeros((STREAMS, TAPS, CH), values.dtype)
    vals_pad = jnp.concatenate([zero_rows, values], axis=1)
    cot_pad = jnp.concatenate([cotangent, zero_rows], axis=1)
    filler = jnp.full((STREAMS, TAPS), -1, jnp.int32)
    ids_front = jnp.concatenate([filler, seg_ids.astype(jnp.int32)], axis=1)
    ids_back = jnp.concatenate([seg_ids.astype(jnp.int32), filler], axis=1)
    blocks = SEQ // TOK_DEV
    zero_i = jnp.zeros((), jnp.int32)

    def one(carry, index):
        fgrad, sgrad = carry
        stream = (index // blocks).astype(jnp.int32)
        start = (index % blocks * TOK_DEV).astype(jnp.int32)
        vals_ext = lax.dynamic_slice(vals_pad, (stream, start, zero_i), (1, width, CH))[0].astype(jnp.float32)
        cot_ext = lax.dynamic_slice(cot_pad, (stream, start, zero_i), (1, width, CH))[0].astype(jnp.float32)
        own_vals = vals_ext[TAPS:]
        own_cot = cot_ext[:TOK_DEV]
        own_ids = lax.dynamic_slice(seg_ids.astype(jnp.int32), (stream, start), (1, TOK_DEV))[0]
        prev_ids = lax.dynamic_slice(ids_front, (stream, start), (1, width))[0]
        next_ids = lax.dynamic_slice(ids_back, (stream, start), (1, width))[0]
        mask_prev = (own_ids[:, None] == prev_ids[None, :]).astype(jnp.float32)
        mask_next = (own_ids[:, None] == next_ids[None, :]).astype(jnp.float32)
        vals_g = vals_ext.reshape(width, GROUPS, GSIZE)
        cot_g = cot_ext.reshape(width, GROUPS, GSIZE)
        conv = jnp.einsum('gts,sgc->tgc', forward * mask_prev[None], vals_g).reshape(TOK_DEV, CH)
        mixed = (conv + skip[None, :] * own_vals).astype(jnp.bfloat16)
        adjoint = jnp.einsum('gtr,rgc->tgc', backward * mask_next[None], cot_g).reshape(TOK_DEV, CH)
        grad_vals = (adjoint + skip[None, :] * own_cot).astype(jnp.bfloat16)
        prod = jnp.einsum('tgc,sgc->gts', own_cot.reshape(TOK_DEV, GROUPS, GSIZE), vals_g) * mask_prev[None]
        fgrad = fgrad + diagonals(prod, TAPS)
        sgrad = sgrad + lax.optimization_barrier(jnp.sum(own_cot * own_vals, axis=0))
        return ((fgrad, sgrad), (mixed, grad_vals))
    init = (jnp.zeros((GROUPS, TAPS), jnp.float32), jnp.zeros((CH,), jnp.float32))
    (fgrad, sgrad), (mixed, grad_vals) = lax.scan(one, init, jnp.arange(STREAMS * blocks, dtype=jnp.int32))
    mixed = mixed.reshape(STREAMS, SEQ, CH)
    grad_vals = grad_vals.reshape(STREAMS, SEQ, CH)
    fgrad = fgrad / jnp.sqrt(jnp.float32(STREAMS * SEQ * GSIZE))
    sgrad = sgrad / jnp.sqrt(jnp.float32(STREAMS * SEQ))
    return (mixed, grad_vals, fgrad, sgrad)
```

```python
import functools

import jax
import jax.numpy as jnp
from jax import lax
from jax.experimental import pallas as pl
from jax.experimental.pallas import tpu as pltpu
from jax.sharding import PartitionSpec as P

MESH = pl.DeviceIdType.MESH
F32 = jnp.float32
BF16 = jnp.bfloat16
LANES = 128
CHUNKS = 4
PARTS = 8
ROWS_Y = 8
ROWS_Z = 12
PACK = 40


def signal_all(peers):
    barrier = pltpu.get_barrier_semaphore()
    for peer in peers:
        pl.semaphore_signal(barrier, inc=1, device_id=peer, device_id_type=MESH)
    pl.semaphore_wait(barrier, len(peers))


def share_kernel(filt_ref, skip_ref, ids_ref, filt_all, skip_all, ids_all, f_buf, s_buf, i_buf, send, recv):
    ctx = lax.axis_index("ctx")
    me = lax.axis_index("fsdp")
    n = lax.axis_size("ctx")
    peers = [(ctx, lax.rem(me + k, PARTS)) for k in range(1, PARTS)]
    after = (lax.rem(ctx + 1, n), me)
    before = (lax.rem(ctx + n - 1, n), me)
    signal_all(peers + [after, before])
    copies = []
    for slot, peer in ((0, after), (2, before)):
        copies.append(pltpu.make_async_remote_copy(
            src_ref=ids_ref, dst_ref=i_buf.at[slot], send_sem=send.at[2, slot], recv_sem=recv.at[2, slot],
            device_id=peer, device_id_type=MESH))
    for k in range(1, PARTS):
        peer = peers[k - 1]
        copies.append(pltpu.make_async_remote_copy(
            src_ref=filt_ref, dst_ref=f_buf.at[k], send_sem=send.at[0, k], recv_sem=recv.at[0, k],
            device_id=peer, device_id_type=MESH))
        copies.append(pltpu.make_async_remote_copy(
            src_ref=skip_ref, dst_ref=s_buf.at[k], send_sem=send.at[1, k], recv_sem=recv.at[1, k],
            device_id=peer, device_id_type=MESH))
    for copy in copies:
        copy.start()
    filt_all[me] = filt_ref[...]
    skip_all[me] = skip_ref[...]
    for copy in copies:
        copy.wait()
    for k in range(1, PARTS):
        owner = lax.rem(me + PARTS - k, PARTS)
        filt_all[owner] = f_buf[k]
        skip_all[owner] = s_buf[k]
    none = jnp.full((1, LANES), -1, jnp.int32)
    ids_all[0] = jnp.where(ctx == 0, none, i_buf[0])
    ids_all[1] = ids_ref[...]
    ids_all[2] = jnp.where(ctx == n - 1, none, i_buf[2])


def share(filters, skip, ids):
    rows = filters.shape[0]
    vm = pl.BlockSpec(memory_space=pltpu.VMEM)
    return pl.pallas_call(
        share_kernel,
        out_shape=(
            jax.ShapeDtypeStruct((PARTS, rows, LANES), BF16),
            jax.ShapeDtypeStruct((PARTS, 4, LANES), BF16),
            jax.ShapeDtypeStruct((3, 1, LANES), jnp.int32),
        ),
        in_specs=[vm] * 3,
        out_specs=(vm, vm, vm),
        scratch_shapes=[
            pltpu.VMEM((PARTS, rows, LANES), BF16),
            pltpu.VMEM((PARTS, 4, LANES), BF16),
            pltpu.VMEM((3, 1, LANES), jnp.int32),
            pltpu.SemaphoreType.DMA((3, PARTS)),
            pltpu.SemaphoreType.DMA((3, PARTS)),
        ],
        compiler_params=pltpu.CompilerParams(collective_id=0, has_side_effects=True),
        name="share",
    )(filters, skip, ids)


def conv_kernel(filt_ref, skip_ref, ids_ref, val_ref, vprev_ref, cot_ref, cnext_ref, *rest):
    mix_ref, gv_ref, gf_ref, gs_ref, bmask, fmask, lhs_a, lhs_b, lhs_c = rest[-9:]
    step = pl.program_id(0)
    row = lax.broadcasted_iota(jnp.int32, (LANES, LANES), 0)
    col = lax.broadcasted_iota(jnp.int32, (LANES, LANES), 1)

    @pl.when(step == 0)
    def _():
        own = jnp.broadcast_to(ids_ref[1].astype(F32), (LANES, LANES))
        mine = own.T
        prev = jnp.broadcast_to(ids_ref[0].astype(F32), (LANES, LANES))
        later = jnp.broadcast_to(ids_ref[2].astype(F32), (LANES, LANES))
        low = jnp.where((col <= row) & (own == mine), 1.0, 0.0)
        up = jnp.where((col > row) & (prev == mine), 1.0, 0.0)
        fmask[0] = low
        fmask[1] = up
        bmask[0] = low.astype(BF16)
        bmask[1] = up.astype(BF16)
        bmask[2] = jnp.where((col >= row) & (own == mine), 1.0, 0.0).astype(BF16)
        bmask[3] = jnp.where((col < row) & (later == mine), 1.0, 0.0).astype(BF16)

    sub = lax.broadcasted_iota(jnp.int32, (8, LANES), 0)
    lane = lax.broadcasted_iota(jnp.int32, (8, LANES), 1)
    back = (sub - lane) & (LANES - 1)
    ahead = (lane - sub) & (LANES - 1)
    group = lax.shift_right_logical(col, 4)
    filt = filt_ref[...].astype(F32)
    val = val_ref[...]
    cot = cot_ref[...]
    for g in range(8):
        taps = jnp.broadcast_to(filt[g : g + 1], (8, LANES))
        fwd = jnp.take_along_axis(taps, back, axis=1)
        bwd = jnp.take_along_axis(taps, ahead, axis=1)
        fwd = jnp.concatenate([fwd] + [pltpu.roll(fwd, 8 * a, 1) for a in range(1, 16)], axis=0).astype(BF16)
        bwd = jnp.concatenate([bwd] + [pltpu.roll(bwd, 8 * a, 1) for a in range(1, 16)], axis=0).astype(BF16)
        rows = pl.ds(g * LANES, LANES)
        lhs_a[rows, 0:LANES] = fwd * bmask[0]
        lhs_a[rows, LANES:] = fwd * bmask[1]
        lhs_b[rows, 0:LANES] = bwd * bmask[2]
        lhs_b[rows, LANES:] = bwd * bmask[3]
        lhs_c[rows, :] = jnp.where(group == g, cot, jnp.zeros_like(cot))
    v_ext = jnp.concatenate([val, vprev_ref[...]], axis=0)
    c_ext = jnp.concatenate([cot, cnext_ref[...]], axis=0)
    conv = jnp.dot(lhs_a[...], v_ext, preferred_element_type=F32)
    adj = jnp.dot(lhs_b[...], c_ext, preferred_element_type=F32)
    prod = lax.dot_general(lhs_c[...], v_ext, (((1,), (1,)), ((), ())), preferred_element_type=F32)
    conv_out = conv[0:LANES]
    adj_out = adj[0:LANES]
    for g in range(1, 8):
        part = slice(g * LANES, (g + 1) * LANES)
        conv_out = jnp.where(group == g, conv[part], conv_out)
        adj_out = jnp.where(group == g, adj[part], adj_out)
    skip = skip_ref[0].astype(F32)
    vf = val.astype(F32)
    cf = cot.astype(F32)
    mix_ref[...] = (conv_out + skip * vf).astype(BF16)
    gv_ref[...] = (adj_out + skip * cf).astype(BF16)
    gs_ref[0] = jnp.sum(vf * cf, axis=0, keepdims=True)
    sums = []
    for g in range(8):
        part = prod[g * LANES : (g + 1) * LANES]
        kept = part[:, :LANES] * fmask[0] + part[:, LANES:] * fmask[1]
        total = kept[0:8]
        for a in range(1, 16):
            total = total + pltpu.roll(kept[8 * a : 8 * a + 8], LANES - 8 * a, 1)
        total = jnp.take_along_axis(total, back, axis=1)
        sums.append(jnp.sum(total, axis=0, keepdims=True))
    gf_ref[...] = jnp.concatenate(sums, axis=0)


def conv_chunk(index, filt, skip, ids, values, vprev, cot, cnext, bufs):
    rows, channels = values.shape
    blocks = channels // LANES // CHUNKS
    base = index * blocks
    wide = lambda i: (0, base + i)
    local = lambda i: (0, i)
    in_specs = [
        pl.BlockSpec((8, LANES), lambda i: (base + i, 0)),
        pl.BlockSpec((1, 1, LANES), lambda i: (base + i, 0, 0)),
        pl.BlockSpec((3, 1, LANES), lambda i: (0, 0, 0)),
        pl.BlockSpec((rows, LANES), wide),
        pl.BlockSpec((rows, LANES), local),
        pl.BlockSpec((rows, LANES), wide),
        pl.BlockSpec((rows, LANES), local),
    ] + [pl.BlockSpec(memory_space=pl.ANY)] * len(bufs)
    out_specs = (
        pl.BlockSpec((rows, LANES), wide),
        pl.BlockSpec((rows, LANES), wide),
        pl.BlockSpec((8, LANES), lambda i: (i, 0)),
        pl.BlockSpec((1, 1, LANES), lambda i: (i, 0, 0)),
    )
    return pl.pallas_call(
        conv_kernel,
        grid=(blocks,),
        in_specs=in_specs,
        out_specs=out_specs,
        out_shape=(
            jax.ShapeDtypeStruct((rows, channels), BF16),
            jax.ShapeDtypeStruct((rows, channels), BF16),
            jax.ShapeDtypeStruct((blocks * 8, LANES), F32),
            jax.ShapeDtypeStruct((blocks, 1, LANES), F32),
        ),
        scratch_shapes=[
            pltpu.VMEM((4, LANES, LANES), BF16),
            pltpu.VMEM((2, LANES, LANES), F32),
            pltpu.VMEM((8 * LANES, 2 * LANES), BF16),
            pltpu.VMEM((8 * LANES, 2 * LANES), BF16),
            pltpu.VMEM((8 * LANES, LANES), BF16),
        ],
        input_output_aliases={7 + k: k for k in range(len(bufs))},
        cost_estimate=pl.CostEstimate(flops=blocks * 8 * 200_000_000, bytes_accessed=2**20, transcendentals=0),
        name=f"conv_{index}",
    )(filt, skip, ids, values, vprev, cot, cnext, *bufs)


def total_kernel(scales, *refs):
    gf_refs, gs_refs = refs[:CHUNKS], refs[CHUNKS : 2 * CHUNKS]
    f_out, s_out, pack, buf_x, buf_z, buf_y, part, send, recv_x, recv_z, recv_y = refs[2 * CHUNKS :]
    ctx = lax.axis_index("ctx")
    me = lax.axis_index("fsdp")
    z, y = ctx // ROWS_Y, lax.rem(ctx, ROWS_Y)
    on_x = [(ctx, lax.rem(me + k, PARTS)) for k in range(1, PARTS)]
    on_z = [(lax.rem(z + k, ROWS_Z) * ROWS_Y + y, me) for k in range(1, ROWS_Z)]
    on_y = [(z * ROWS_Y + lax.rem(y + k, ROWS_Y), me) for k in range(1, ROWS_Y)]
    per = PARTS // CHUNKS
    for c in range(CHUNKS):
        for p in range(per):
            pack[c * per + p, 0:32] = gf_refs[c][32 * p : 32 * p + 32]
            pack[c * per + p, 32:PACK] = jnp.zeros((PACK - 32, LANES), F32)
            for r in range(4):
                pack[c * per + p, 32 + r : 33 + r] = gs_refs[c][4 * p + r]
    signal_all(on_x + on_z + on_y)

    def exchange(source_of, peers, mine, buf, recv, own):
        copies = []
        for k, peer in enumerate(peers):
            copies.append(pltpu.make_async_remote_copy(
                src_ref=source_of(peer), dst_ref=buf.at[mine], send_sem=send.at[k], recv_sem=recv.at[mine],
                device_id=peer, device_id_type=MESH))
            copies[-1].start()
        buf[mine] = own
        n = len(peers) + 1
        for k in range(1, n):
            slot = lax.rem(mine + k, n)
            pltpu.make_async_remote_copy(
                src_ref=buf.at[slot], dst_ref=buf.at[slot], send_sem=send.at[k - 1], recv_sem=recv.at[slot],
                device_id=peers[k - 1], device_id_type=MESH).wait_recv()
        for copy in copies:
            copy.wait_send()
        total = buf[0]
        for k in range(1, n):
            total = total + buf[k]
        return total

    one = exchange(lambda peer: pack.at[peer[1]], on_x, me, buf_x, recv_x, pack[me])
    part[0] = one
    two = exchange(lambda peer: part.at[0], on_z, z, buf_z, recv_z, one)
    part[1] = two
    three = exchange(lambda peer: part.at[1], on_y, y, buf_y, recv_y, two)
    f_out[...] = three[0:32] / jnp.sqrt(F32(scales[0]))
    s_out[...] = three[32:36] / jnp.sqrt(F32(scales[1]))


def totals(gfs, gss, scales):
    vm = pl.BlockSpec(memory_space=pltpu.VMEM)
    return pl.pallas_call(
        functools.partial(total_kernel, scales),
        out_shape=(jax.ShapeDtypeStruct((32, LANES), F32), jax.ShapeDtypeStruct((4, LANES), F32)),
        in_specs=[vm] * (2 * CHUNKS),
        out_specs=(vm, vm),
        scratch_shapes=[
            pltpu.VMEM((PARTS, PACK, LANES), F32),
            pltpu.VMEM((PARTS, PACK, LANES), F32),
            pltpu.VMEM((ROWS_Z, PACK, LANES), F32),
            pltpu.VMEM((ROWS_Y, PACK, LANES), F32),
            pltpu.VMEM((2, PACK, LANES), F32),
            pltpu.SemaphoreType.DMA((ROWS_Z,)),
            pltpu.SemaphoreType.DMA((PARTS,)),
            pltpu.SemaphoreType.DMA((ROWS_Z,)),
            pltpu.SemaphoreType.DMA((ROWS_Y,)),
        ],
        compiler_params=pltpu.CompilerParams(collective_id=1, has_side_effects=True),
        name="totals",
    )(*gfs, *gss)


def shards(values, cotangent, seg_ids, filters, skip_gain):
    vals, cot = values[0], cotangent[0]
    rows, channels = vals.shape
    n = lax.axis_size("ctx")
    ahead = [(i, i + 1) for i in range(n - 1)]
    behind = [(i + 1, i) for i in range(n - 1)]
    width = channels // CHUNKS
    vprev, cnext = [], []
    for c in range(CHUNKS):
        cut = slice(c * width, (c + 1) * width)
        vprev.append(lax.ppermute(vals[:, cut], "ctx", ahead))
        cnext.append(lax.ppermute(cot[:, cut], "ctx", behind))
    filt, skip, ids = share(filters, skip_gain.reshape(4, LANES), seg_ids)
    filt = filt.reshape(-1, LANES)
    skip = skip.reshape(channels // LANES, 1, LANES)
    bufs, gfs, gss = (), [], []
    for c in range(CHUNKS):
        mixed, grad, gf, gs = conv_chunk(c, filt, skip, ids, vals, vprev[c], cot, cnext[c], bufs)
        bufs = (mixed, grad)
        gfs.append(gf)
        gss.append(gs)
    streams = lax.axis_size("fsdp")
    length = rows * n
    total_f, total_s = totals(gfs, gss, (streams * length * 16, streams * length))
    return (mixed[None], grad[None], total_f, total_s.reshape(-1))


def solution(mesh):
    placed = (P("fsdp", "ctx", None), P("fsdp", "ctx", None), P("fsdp", "ctx"), P("fsdp", None), P("fsdp"))
    return jax.shard_map(
        shards,
        mesh=mesh,
        in_specs=placed,
        out_specs=(P("fsdp", "ctx", None), P("fsdp", "ctx", None), P("fsdp", None), P("fsdp")),
        check_vma=False,
    )
```

```python
import jax
import jax.numpy as jnp
from jax import lax
from jax.experimental import pallas as pl
from jax.experimental.pallas import tpu as pltpu
from jax.sharding import PartitionSpec as P

MESH = pl.DeviceIdType.MESH
F32 = jnp.float32
BF16 = jnp.bfloat16
LANES = 128
CHUNKS = 8
PARTS = 8
ROWS_Y = 8
ROWS_Z = 12
PACK = 40
PER = 4
HALF = CHUNKS // 2
ORDER_V = (0, 1, 2, 3, 4, 5, 6, 7)
ORDER_C = (4, 5, 6, 7, 0, 1, 2, 3)
ORDER_A = (0, 4, 1, 5, 2, 6, 3, 7)
SEGMENTS = ((0, 2), (2, 5), (5, 8))


def columns(block):
    return pl.ds(pl.multiple_of(block * LANES, LANES), LANES)


def set_masks(ids, bmask, fmask):
    row = lax.broadcasted_iota(jnp.int32, (LANES, LANES), 0)
    col = lax.broadcasted_iota(jnp.int32, (LANES, LANES), 1)
    prev, own, later = [jnp.broadcast_to(x.astype(F32), (LANES, LANES)) for x in ids]
    mine = own.T
    kept = (
        (col <= row) & (own == mine),
        (col > row) & (prev == mine),
        (col >= row) & (own == mine),
        (col < row) & (later == mine),
    )
    for k in range(4):
        mask = jnp.where(kept[k], 1.0, 0.0)
        fmask[k] = mask
        bmask[k] = mask.astype(BF16)


def filter_block(chunk, inner, left, own, halo, first, fmask, pack, sums):
    cols = columns(chunk * PER + inner)
    group = lax.shift_right_logical(lax.broadcasted_iota(jnp.int32, (LANES, LANES), 1), 4)
    x = left[:, cols]
    y = own[:, cols]
    lhs = jnp.concatenate([jnp.where(group == g, x, jnp.zeros_like(x)) for g in range(8)], axis=0)
    rhs = jnp.concatenate([y, halo[:, cols]], axis=0)
    prod = lax.dot_general(lhs, rhs, (((1,), (1,)), ((), ())), preferred_element_type=F32)
    for g in range(8):
        part = prod[g * LANES : (g + 1) * LANES]
        kept = part[:, :LANES] * fmask[first] + part[:, LANES:] * fmask[first + 1]
        total = kept[0:8]
        for a in range(1, 16):
            total = total + pltpu.roll(kept[8 * a : 8 * a + 8], LANES - 8 * a, 1)
        sums[8 * g : 8 * g + 8] = total
    total = sums[pl.ds(0, 8, stride=8)]
    for b in range(1, 8):
        total = total + pltpu.roll(sums[pl.ds(b, 8, stride=8)], LANES - b, 1)
    pack[chunk, pl.ds(pl.multiple_of(inner * 8, 8), 8)] = total
    pack[chunk, pl.ds(32 + inner, 1)] = jnp.sum(x.astype(F32) * y.astype(F32), axis=0, keepdims=True)


def build(block, filt, flip, bmask, lhs):
    rows = pl.ds(pl.multiple_of(block * 8, 8), 8)
    taps = filt[rows]
    mirror = flip[rows]
    for g in range(8):
        spot = pl.ds(g * LANES, LANES)
        for source, first in ((mirror, 0), (taps, 2)):
            base = pltpu.roll(jnp.broadcast_to(source[g : g + 1], (8, LANES)), 0, 1, stride=1, stride_axis=0)
            circ = jnp.concatenate([base] + [pltpu.roll(base, 8 * a, 1) for a in range(1, 16)], axis=0).astype(BF16)
            lhs[first, spot] = circ * bmask[first]
            lhs[first + 1, spot] = circ * bmask[first + 1]


def apply(block, lhs, skips, vals, vprev, cot, cnext, mix, grad):
    cols = columns(block)
    group = lax.shift_right_logical(lax.broadcasted_iota(jnp.int32, (LANES, LANES), 1), 4)
    skip = skips[block // PER, pl.ds(lax.rem(block, PER), 1)]
    for first, own, halo, out in ((0, vals, vprev, mix), (2, cot, cnext, grad)):
        mine = own[:, cols]
        rhs = jnp.concatenate([mine, halo[:, cols]], axis=0)
        full = jnp.dot(jnp.concatenate([lhs[first], lhs[first + 1]], axis=1), rhs, preferred_element_type=F32)
        kept = full[0:LANES]
        for g in range(1, 8):
            kept = jnp.where(group == g, full[g * LANES : (g + 1) * LANES], kept)
        out[:, cols] = (kept + skip * mine.astype(F32)).astype(BF16)


def kernel(
    vals_hbm, cot_hbm, filt_ref, skip_ref, ids_ref, mix_hbm, grad_hbm, f_out, s_out,
    vals, cot, vprev, cnext, mix, grad, filt_all, skip_all, ids_buf, filt, flip, skips, bmask, fmask,
    lhs_a, lhs_b, sums_a, sums_b, pack, buf_x, buf_y, buf_z, part,
    load, send_v, recv_v, send_c, recv_c, send_f, recv_f, send_s, recv_s, send_i, recv_i,
    send_x, recv_x, send_y, recv_y, send_z, recv_z,
):
    ctx = lax.axis_index("ctx")
    me = lax.axis_index("fsdp")
    n = lax.axis_size("ctx")
    z, y = ctx // ROWS_Y, lax.rem(ctx, ROWS_Y)
    on_x = [(ctx, lax.rem(me + k, PARTS)) for k in range(1, PARTS)]
    on_z = [(lax.rem(z + k, ROWS_Z) * ROWS_Y + y, me) for k in range(1, ROWS_Z)]
    on_y = [(z * ROWS_Y + lax.rem(y + k, ROWS_Y), me) for k in range(1, ROWS_Y)]
    after = (lax.rem(ctx + 1, n), me)
    before = (lax.rem(ctx + n - 1, n), me)

    loads = [
        pltpu.make_async_copy(vals_hbm, vals, load.at[0]),
        pltpu.make_async_copy(cot_hbm, cot, load.at[1]),
    ]
    for copy in loads:
        copy.start()

    barrier = pltpu.get_barrier_semaphore()
    greeted = [after, before] + on_x + on_y + on_z
    for peer in greeted:
        pl.semaphore_signal(barrier, inc=1, device_id=peer, device_id_type=MESH)
    pl.semaphore_wait(barrier, len(greeted))

    def remote(src, dst, send, recv, peer):
        return pltpu.make_async_remote_copy(
            src_ref=src, dst_ref=dst, send_sem=send, recv_sem=recv, device_id=peer, device_id_type=MESH
        )

    small = [
        remote(ids_ref, ids_buf.at[0], send_i.at[0], recv_i.at[0], after),
        remote(ids_ref, ids_buf.at[1], send_i.at[1], recv_i.at[1], before),
    ]
    for copy in small:
        copy.start()
    width = PER * LANES
    v_copies, c_copies = {}, {}
    for k in range(CHUNKS):
        cut = pl.ds(ORDER_V[k] * width, width)
        v_copies[ORDER_V[k]] = remote(vals_hbm.at[:, cut], vprev.at[:, cut], send_v.at[k], recv_v.at[k], after)
        v_copies[ORDER_V[k]].start()
        cut = pl.ds(ORDER_C[k] * width, width)
        c_copies[ORDER_C[k]] = remote(cot_hbm.at[:, cut], cnext.at[:, cut], send_c.at[k], recv_c.at[k], before)
        c_copies[ORDER_C[k]].start()

    def spread(source_of, peers, mine, buf, send, recv, own):
        copies = []
        for k, peer in enumerate(peers):
            copies.append(remote(source_of(peer), buf.at[mine], send.at[k], recv.at[mine], peer))
            copies[-1].start()
        buf[mine] = own
        return copies

    def gathered(copies, peers, mine, buf, send, recv):
        count = len(peers) + 1
        for k in range(1, count):
            slot = lax.rem(mine + k, count)
            remote(buf.at[slot], buf.at[slot], send.at[k - 1], recv.at[slot], peers[k - 1]).wait_recv()
        for copy in copies:
            copy.wait_send()

    def summed(buf, count):
        total = buf[0]
        for k in range(1, count):
            total = total + buf[k]
        return total

    f_copies = spread(lambda peer: filt_ref, on_x, me, filt_all, send_f, recv_f, filt_ref[...])
    s_copies = spread(lambda peer: skip_ref, on_x, me, skip_all, send_s, recv_s, skip_ref[...])
    for k in range(PARTS):
        pack[k, 32:PACK] = jnp.zeros((PACK - 32, LANES), F32)

    for copy in small:
        copy.wait()
    none = jnp.full((1, LANES), -1, jnp.int32)
    set_masks(
        (jnp.where(ctx == 0, none, ids_buf[0]), ids_ref[...], jnp.where(ctx == n - 1, none, ids_buf[1])),
        bmask, fmask,
    )
    for copy in loads:
        copy.wait()

    for chunk in ORDER_A:
        if chunk < HALF:
            v_copies[chunk].wait_recv()
            refs = (cot, vals, vprev, 0)
        else:
            c_copies[chunk].wait_recv()
            refs = (vals, cot, cnext, 2)

        def two(j, carry, chunk=chunk, refs=refs):
            filter_block(chunk, 2 * j, *refs, fmask, pack, sums_a)
            filter_block(chunk, 2 * j + 1, *refs, fmask, pack, sums_b)
            return carry

        lax.fori_loop(0, PER // 2, two, 0)

    x_copies = spread(lambda peer: pack.at[peer[1]], on_x, me, buf_x, send_x, recv_x, pack[me])

    gathered(f_copies, on_x, me, filt_all, send_f, recv_f)
    gathered(s_copies, on_x, me, skip_all, send_s, recv_s)
    row = lax.broadcasted_iota(jnp.int32, (LANES, LANES), 0)
    col = lax.broadcasted_iota(jnp.int32, (LANES, LANES), 1)
    turn = jnp.where(((row + col) & (LANES - 1)) == 0, 1.0, 0.0).astype(BF16)
    for k in range(PARTS):
        skips[k] = skip_all[k].astype(F32)
        filt[32 * k : 32 * k + 32] = filt_all[k].astype(F32)
        flip[32 * k : 32 * k + 32] = jnp.dot(filt_all[k], turn, preferred_element_type=F32)
    for chunk in range(CHUNKS):
        if chunk < HALF:
            c_copies[chunk].wait_recv()
        else:
            v_copies[chunk].wait_recv()

    build(0, filt, flip, bmask, lhs_a)
    last = CHUNKS * PER - 1
    stores = []

    def segment(first, stop):
        def two(j, carry):
            block = first * PER + 2 * j
            build(block + 1, filt, flip, bmask, lhs_b)
            apply(block, lhs_a, skips, vals, vprev, cot, cnext, mix, grad)
            build(jnp.minimum(block + 2, last), filt, flip, bmask, lhs_a)
            apply(block + 1, lhs_b, skips, vals, vprev, cot, cnext, mix, grad)
            return carry

        lax.fori_loop(0, (stop - first) * PER // 2, two, 0)
        cut = pl.ds(first * width, (stop - first) * width)
        k = 2 + len(stores)
        for source, target in ((mix, mix_hbm), (grad, grad_hbm)):
            stores.append(pltpu.make_async_copy(source.at[:, cut], target.at[:, cut], load.at[k]))
            stores[-1].start()
            k += 1

    segment(*SEGMENTS[0])
    gathered(x_copies, on_x, me, buf_x, send_x, recv_x)
    part[0] = summed(buf_x, PARTS)
    y_copies = spread(lambda peer: part.at[0], on_y, y, buf_y, send_y, recv_y, part[0])
    segment(*SEGMENTS[1])
    gathered(y_copies, on_y, y, buf_y, send_y, recv_y)
    part[1] = summed(buf_y, ROWS_Y)
    z_copies = spread(lambda peer: part.at[1], on_z, z, buf_z, send_z, recv_z, part[1])
    segment(*SEGMENTS[2])
    gathered(z_copies, on_z, z, buf_z, send_z, recv_z)
    total = summed(buf_z, ROWS_Z)
    f_out[...] = total[0:32]
    s_out[...] = total[32:36]
    for chunk in range(CHUNKS):
        v_copies[chunk].wait_send()
        c_copies[chunk].wait_send()
    for copy in stores:
        copy.wait()


def shards(values, cotangent, seg_ids, filters, skip_gain):
    vals, cot = values[0], cotangent[0]
    rows, channels = vals.shape
    vm = pl.BlockSpec(memory_space=pltpu.VMEM)
    hbm = pl.BlockSpec(memory_space=pl.ANY)
    wide = pltpu.VMEM((rows, channels), BF16)
    dma = pltpu.SemaphoreType.DMA
    groups = channels // 16
    mixed, grad, total_f, total_s = pl.pallas_call(
        kernel,
        out_shape=(
            jax.ShapeDtypeStruct((rows, channels), BF16),
            jax.ShapeDtypeStruct((rows, channels), BF16),
            jax.ShapeDtypeStruct((32, LANES), F32),
            jax.ShapeDtypeStruct((PER, LANES), F32),
        ),
        in_specs=[hbm, hbm, vm, vm, vm],
        out_specs=(hbm, hbm, vm, vm),
        scratch_shapes=[
            wide, wide, wide, wide, wide, wide,
            pltpu.VMEM((PARTS, 32, LANES), BF16),
            pltpu.VMEM((PARTS, PER, LANES), BF16),
            pltpu.VMEM((2, 1, LANES), jnp.int32),
            pltpu.VMEM((groups, LANES), F32),
            pltpu.VMEM((groups, LANES), F32),
            pltpu.VMEM((PARTS, PER, LANES), F32),
            pltpu.VMEM((4, LANES, LANES), BF16),
            pltpu.VMEM((4, LANES, LANES), F32),
            pltpu.VMEM((4, 8 * LANES, LANES), BF16),
            pltpu.VMEM((4, 8 * LANES, LANES), BF16),
            pltpu.VMEM((64, LANES), F32),
            pltpu.VMEM((64, LANES), F32),
            pltpu.VMEM((PARTS, PACK, LANES), F32),
            pltpu.VMEM((PARTS, PACK, LANES), F32),
            pltpu.VMEM((ROWS_Y, PACK, LANES), F32),
            pltpu.VMEM((ROWS_Z, PACK, LANES), F32),
            pltpu.VMEM((2, PACK, LANES), F32),
            dma((8,)), dma((8,)), dma((8,)), dma((8,)), dma((8,)), dma((8,)), dma((8,)),
            dma((8,)), dma((8,)), dma((2,)), dma((2,)),
            dma((8,)), dma((8,)), dma((8,)), dma((8,)), dma((12,)), dma((12,)),
        ],
        compiler_params=pltpu.CompilerParams(collective_id=0, has_side_effects=True),
        name="layer",
    )(vals, cot, filters, skip_gain.reshape(PER, LANES), seg_ids)
    streams = lax.axis_size("fsdp")
    length = rows * lax.axis_size("ctx")
    mirrored = jnp.concatenate([total_f[:, :1], total_f[:, :0:-1]], axis=1)
    total_f = jnp.where(lax.axis_index("fsdp") < HALF, mirrored, total_f)
    total_f = total_f / jnp.sqrt(F32(streams * length * 16))
    total_s = total_s / jnp.sqrt(F32(streams * length))
    return (mixed[None], grad[None], total_f, total_s.reshape(-1))


def solution(mesh):
    placed = (P("fsdp", "ctx", None), P("fsdp", "ctx", None), P("fsdp", "ctx"), P("fsdp", None), P("fsdp"))
    return jax.shard_map(
        shards,
        mesh=mesh,
        in_specs=placed,
        out_specs=(P("fsdp", "ctx", None), P("fsdp", "ctx", None), P("fsdp", None), P("fsdp")),
        check_vma=False,
    )
```

```python
import jax
import jax.numpy as jnp
from jax import lax
from jax.experimental import pallas as pl
from jax.experimental.pallas import tpu as pltpu
from jax.sharding import PartitionSpec as P

MESH = pl.DeviceIdType.MESH
F32 = jnp.float32
BF16 = jnp.bfloat16
LANES = 128
CHUNKS = 8
PARTS = 8
ROWS_Y = 8
ROWS_Z = 12
PACK = 40
PER = 4
HALF = CHUNKS // 2
ORDER_V = (0, 1, 2, 3, 4, 5, 6, 7)
ORDER_C = (4, 5, 6, 7, 0, 1, 2, 3)
ORDER_A = (0, 4, 1, 5, 2, 6, 3, 7)
SEGMENTS = ((0, 2), (2, 5), (5, 8))


def columns(block):
    return pl.ds(pl.multiple_of(block * LANES, LANES), LANES)


def set_masks(ids, bmask, fmask):
    row = lax.broadcasted_iota(jnp.int32, (LANES, LANES), 0)
    col = lax.broadcasted_iota(jnp.int32, (LANES, LANES), 1)
    prev, own, later = [jnp.broadcast_to(x.astype(F32), (LANES, LANES)) for x in ids]
    mine = own.T
    kept = (
        (col <= row) & (own == mine),
        (col > row) & (prev == mine),
        (col >= row) & (own == mine),
        (col < row) & (later == mine),
    )
    for k in range(4):
        mask = jnp.where(kept[k], 1.0, 0.0)
        fmask[k] = mask
        bmask[k] = mask.astype(BF16)


def filter_block(chunk, inner, left, own, halo, first, fmask, pack, sums):
    cols = columns(chunk * PER + inner)
    group = lax.shift_right_logical(lax.broadcasted_iota(jnp.int32, (LANES, LANES), 1), 4)
    x = left[:, cols]
    y = own[:, cols]
    lhs = jnp.concatenate([jnp.where(group == g, x, jnp.zeros_like(x)) for g in range(8)], axis=0)
    rhs = jnp.concatenate([y, halo[:, cols]], axis=0)
    prod = lax.dot_general(lhs, rhs, (((1,), (1,)), ((), ())), preferred_element_type=F32)
    for g in range(8):
        part = prod[g * LANES : (g + 1) * LANES]
        kept = part[:, :LANES] * fmask[first] + part[:, LANES:] * fmask[first + 1]
        total = kept[0:8]
        for a in range(1, 16):
            total = total + pltpu.roll(kept[8 * a : 8 * a + 8], LANES - 8 * a, 1)
        sums[8 * g : 8 * g + 8] = total
    total = sums[pl.ds(0, 8, stride=8)]
    for b in range(1, 8):
        total = total + pltpu.roll(sums[pl.ds(b, 8, stride=8)], LANES - b, 1)
    pack[chunk, pl.ds(pl.multiple_of(inner * 8, 8), 8)] = total
    pack[chunk, pl.ds(32 + inner, 1)] = jnp.sum(x.astype(F32) * y.astype(F32), axis=0, keepdims=True)


def build(block, filt, flip, bmask, lhs):
    rows = pl.ds(pl.multiple_of(block * 8, 8), 8)
    taps = filt[rows]
    mirror = flip[rows]
    for g in range(8):
        spot = pl.ds(g * LANES, LANES)
        for source, first in ((mirror, 0), (taps, 2)):
            base = pltpu.roll(jnp.broadcast_to(source[g : g + 1], (8, LANES)), 0, 1, stride=1, stride_axis=0)
            circ = jnp.concatenate([base] + [pltpu.roll(base, 8 * a, 1) for a in range(1, 16)], axis=0).astype(BF16)
            lhs[first, spot] = circ * bmask[first]
            lhs[first + 1, spot] = circ * bmask[first + 1]


def apply(block, lhs, skips, vals, vprev, cot, cnext, mix, grad):
    cols = columns(block)
    group = lax.shift_right_logical(lax.broadcasted_iota(jnp.int32, (LANES, LANES), 1), 4)
    skip = skips[block // PER, pl.ds(lax.rem(block, PER), 1)]
    for first, own, halo, out in ((0, vals, vprev, mix), (2, cot, cnext, grad)):
        mine = own[:, cols]
        rhs = jnp.concatenate([mine, halo[:, cols]], axis=0)
        full = jnp.dot(jnp.concatenate([lhs[first], lhs[first + 1]], axis=1), rhs, preferred_element_type=F32)
        kept = full[0:LANES]
        for g in range(1, 8):
            kept = jnp.where(group == g, full[g * LANES : (g + 1) * LANES], kept)
        out[:, cols] = (kept + skip * mine.astype(F32)).astype(BF16)


def kernel(
    vals_hbm, cot_hbm, filt_ref, skip_ref, ids_ref, mix_hbm, grad_hbm, f_out, s_out,
    vals, cot, vprev, cnext, mix, grad, filt_all, skip_all, ids_buf, filt, flip, skips, bmask, fmask,
    lhs_a, lhs_b, sums_a, sums_b, pack, buf_x, buf_y, buf_z, part,
    load, send_v, recv_v, send_c, recv_c, send_f, recv_f, send_s, recv_s, send_i, recv_i,
    send_x, recv_x, send_y, recv_y, send_z, recv_z,
):
    ctx = lax.axis_index("ctx")
    me = lax.axis_index("fsdp")
    n = lax.axis_size("ctx")
    z, y = ctx // ROWS_Y, lax.rem(ctx, ROWS_Y)
    on_x = [(ctx, lax.rem(me + k, PARTS)) for k in range(1, PARTS)]
    on_z = [(lax.rem(z + k, ROWS_Z) * ROWS_Y + y, me) for k in range(1, ROWS_Z)]
    on_y = [(z * ROWS_Y + lax.rem(y + k, ROWS_Y), me) for k in range(1, ROWS_Y)]
    after = (lax.rem(ctx + 1, n), me)
    before = (lax.rem(ctx + n - 1, n), me)

    loads = [
        pltpu.make_async_copy(vals_hbm, vals, load.at[0]),
        pltpu.make_async_copy(cot_hbm, cot, load.at[1]),
    ]
    for copy in loads:
        copy.start()

    barrier = pltpu.get_barrier_semaphore()
    greeted = [after, before] + on_x + on_y + on_z
    for peer in greeted:
        pl.semaphore_signal(barrier, inc=1, device_id=peer, device_id_type=MESH)
    pl.semaphore_wait(barrier, len(greeted))

    def remote(src, dst, send, recv, peer):
        return pltpu.make_async_remote_copy(
            src_ref=src, dst_ref=dst, send_sem=send, recv_sem=recv, device_id=peer, device_id_type=MESH
        )

    small = [
        remote(ids_ref, ids_buf.at[0], send_i.at[0], recv_i.at[0], after),
        remote(ids_ref, ids_buf.at[1], send_i.at[1], recv_i.at[1], before),
    ]
    for copy in small:
        copy.start()
    width = PER * LANES
    v_copies, c_copies = {}, {}
    for k in range(CHUNKS):
        cut = pl.ds(ORDER_V[k] * width, width)
        v_copies[ORDER_V[k]] = remote(vals_hbm.at[:, cut], vprev.at[:, cut], send_v.at[k], recv_v.at[k], after)
        v_copies[ORDER_V[k]].start()
        cut = pl.ds(ORDER_C[k] * width, width)
        c_copies[ORDER_C[k]] = remote(cot_hbm.at[:, cut], cnext.at[:, cut], send_c.at[k], recv_c.at[k], before)
        c_copies[ORDER_C[k]].start()

    def spread(source_of, peers, mine, buf, send, recv, own):
        copies = []
        for k, peer in enumerate(peers):
            copies.append(remote(source_of(peer), buf.at[mine], send.at[k], recv.at[mine], peer))
            copies[-1].start()
        buf[mine] = own
        return copies

    def gathered(copies, peers, mine, buf, send, recv):
        count = len(peers) + 1
        for k in range(1, count):
            slot = lax.rem(mine + k, count)
            remote(buf.at[slot], buf.at[slot], send.at[k - 1], recv.at[slot], peers[k - 1]).wait_recv()
        for copy in copies:
            copy.wait_send()

    def summed(buf, count):
        total = buf[0]
        for k in range(1, count):
            total = total + buf[k]
        return total

    f_copies = spread(lambda peer: filt_ref, on_x, me, filt_all, send_f, recv_f, filt_ref[...])
    s_copies = spread(lambda peer: skip_ref, on_x, me, skip_all, send_s, recv_s, skip_ref[...])
    for k in range(PARTS):
        pack[k, 32:PACK] = jnp.zeros((PACK - 32, LANES), F32)

    for copy in small:
        copy.wait()
    none = jnp.full((1, LANES), -1, jnp.int32)
    set_masks(
        (jnp.where(ctx == 0, none, ids_buf[0]), ids_ref[...], jnp.where(ctx == n - 1, none, ids_buf[1])),
        bmask, fmask,
    )
    for copy in loads:
        copy.wait()

    for chunk in ORDER_A:
        if chunk < HALF:
            v_copies[chunk].wait_recv()
            refs = (cot, vals, vprev, 0)
        else:
            c_copies[chunk].wait_recv()
            refs = (vals, cot, cnext, 2)

        def two(j, carry, chunk=chunk, refs=refs):
            filter_block(chunk, 2 * j, *refs, fmask, pack, sums_a)
            filter_block(chunk, 2 * j + 1, *refs, fmask, pack, sums_b)
            return carry

        lax.fori_loop(0, PER // 2, two, 0)

    x_copies = spread(lambda peer: pack.at[peer[1]], on_x, me, buf_x, send_x, recv_x, pack[me])

    gathered(f_copies, on_x, me, filt_all, send_f, recv_f)
    gathered(s_copies, on_x, me, skip_all, send_s, recv_s)
    row = lax.broadcasted_iota(jnp.int32, (LANES, LANES), 0)
    col = lax.broadcasted_iota(jnp.int32, (LANES, LANES), 1)
    turn = jnp.where(((row + col) & (LANES - 1)) == 0, 1.0, 0.0).astype(BF16)
    for k in range(PARTS):
        skips[k] = skip_all[k].astype(F32)
        filt[32 * k : 32 * k + 32] = filt_all[k].astype(F32)
        flip[32 * k : 32 * k + 32] = jnp.dot(filt_all[k], turn, preferred_element_type=F32)
    build(0, filt, flip, bmask, lhs_a)
    last = CHUNKS * PER - 1
    stores = []

    def segment(first, stop):
        for chunk in range(first, stop):
            (c_copies if chunk < HALF else v_copies)[chunk].wait_recv()

        def two(j, carry):
            block = first * PER + 2 * j
            build(block + 1, filt, flip, bmask, lhs_b)
            apply(block, lhs_a, skips, vals, vprev, cot, cnext, mix, grad)
            build(jnp.minimum(block + 2, last), filt, flip, bmask, lhs_a)
            apply(block + 1, lhs_b, skips, vals, vprev, cot, cnext, mix, grad)
            return carry

        lax.fori_loop(0, (stop - first) * PER // 2, two, 0)
        cut = pl.ds(first * width, (stop - first) * width)
        k = 2 + len(stores)
        for source, target in ((mix, mix_hbm), (grad, grad_hbm)):
            stores.append(pltpu.make_async_copy(source.at[:, cut], target.at[:, cut], load.at[k]))
            stores[-1].start()
            k += 1

    segment(*SEGMENTS[0])
    gathered(x_copies, on_x, me, buf_x, send_x, recv_x)
    part[0] = summed(buf_x, PARTS)
    y_copies = spread(lambda peer: part.at[0], on_y, y, buf_y, send_y, recv_y, part[0])
    segment(*SEGMENTS[1])
    gathered(y_copies, on_y, y, buf_y, send_y, recv_y)
    part[1] = summed(buf_y, ROWS_Y)
    z_copies = spread(lambda peer: part.at[1], on_z, z, buf_z, send_z, recv_z, part[1])
    segment(*SEGMENTS[2])
    gathered(z_copies, on_z, z, buf_z, send_z, recv_z)
    total = summed(buf_z, ROWS_Z)
    f_out[...] = total[0:32]
    s_out[...] = total[32:36]
    for chunk in range(CHUNKS):
        v_copies[chunk].wait_send()
        c_copies[chunk].wait_send()
    for copy in stores:
        copy.wait()


def shards(values, cotangent, seg_ids, filters, skip_gain):
    vals, cot = values[0], cotangent[0]
    rows, channels = vals.shape
    vm = pl.BlockSpec(memory_space=pltpu.VMEM)
    hbm = pl.BlockSpec(memory_space=pl.ANY)
    wide = pltpu.VMEM((rows, channels), BF16)
    dma = pltpu.SemaphoreType.DMA
    groups = channels // 16
    mixed, grad, total_f, total_s = pl.pallas_call(
        kernel,
        out_shape=(
            jax.ShapeDtypeStruct((rows, channels), BF16),
            jax.ShapeDtypeStruct((rows, channels), BF16),
            jax.ShapeDtypeStruct((32, LANES), F32),
            jax.ShapeDtypeStruct((PER, LANES), F32),
        ),
        in_specs=[hbm, hbm, vm, vm, vm],
        out_specs=(hbm, hbm, vm, vm),
        scratch_shapes=[
            wide, wide, wide, wide, wide, wide,
            pltpu.VMEM((PARTS, 32, LANES), BF16),
            pltpu.VMEM((PARTS, PER, LANES), BF16),
            pltpu.VMEM((2, 1, LANES), jnp.int32),
            pltpu.VMEM((groups, LANES), F32),
            pltpu.VMEM((groups, LANES), F32),
            pltpu.VMEM((PARTS, PER, LANES), F32),
            pltpu.VMEM((4, LANES, LANES), BF16),
            pltpu.VMEM((4, LANES, LANES), F32),
            pltpu.VMEM((4, 8 * LANES, LANES), BF16),
            pltpu.VMEM((4, 8 * LANES, LANES), BF16),
            pltpu.VMEM((64, LANES), F32),
            pltpu.VMEM((64, LANES), F32),
            pltpu.VMEM((PARTS, PACK, LANES), F32),
            pltpu.VMEM((PARTS, PACK, LANES), F32),
            pltpu.VMEM((ROWS_Y, PACK, LANES), F32),
            pltpu.VMEM((ROWS_Z, PACK, LANES), F32),
            pltpu.VMEM((2, PACK, LANES), F32),
            dma((8,)), dma((8,)), dma((8,)), dma((8,)), dma((8,)), dma((8,)), dma((8,)),
            dma((8,)), dma((8,)), dma((2,)), dma((2,)),
            dma((8,)), dma((8,)), dma((8,)), dma((8,)), dma((12,)), dma((12,)),
        ],
        compiler_params=pltpu.CompilerParams(collective_id=0, has_side_effects=True),
        name="layer",
    )(vals, cot, filters, skip_gain.reshape(PER, LANES), seg_ids)
    streams = lax.axis_size("fsdp")
    length = rows * lax.axis_size("ctx")
    mirrored = jnp.concatenate([total_f[:, :1], total_f[:, :0:-1]], axis=1)
    total_f = jnp.where(lax.axis_index("fsdp") < HALF, mirrored, total_f)
    total_f = total_f / jnp.sqrt(F32(streams * length * 16))
    total_s = total_s / jnp.sqrt(F32(streams * length))
    return (mixed[None], grad[None], total_f, total_s.reshape(-1))


def solution(mesh):
    placed = (P("fsdp", "ctx", None), P("fsdp", "ctx", None), P("fsdp", "ctx"), P("fsdp", None), P("fsdp"))
    return jax.shard_map(
        shards,
        mesh=mesh,
        in_specs=placed,
        out_specs=(P("fsdp", "ctx", None), P("fsdp", "ctx", None), P("fsdp", None), P("fsdp")),
        check_vma=False,
    )
```
